32 devices in a mesh: row: 16 (over z, y, x), col: 2 (over core).
Axes of the slice: x: 2, y: 2, z: 4, core: 2. Of those that a mesh axis runs over, the one named last changes fastest.
Arguments:
- sim_points: float32 [64, 4096], P(None, 'row'), may hold values from -34 to 34
- obs_points: float32 [64, 4096], P(None, ('row', 'col')), may hold values from -16 to 16
- sim_logw: float32 [4096], P('row'), may hold values from -2.5 to 2.5
- obs_logw: float32 [4096], P(('row', 'col')), may hold values from -2.5 to 2.5
Outputs:
- potential_f: float32 [4096], P('row')
- potential_g: float32 [4096], P(('row', 'col'))
- transport_cost: float32 [1], replicated
The draws below stay inside these ranges and needn't reach their ends.
All inputs are finite; a program needn't handle non-finite values.
Results may differ from the reference program's by a relative error of at most 0.0003.
Values sent between devices are 32-bit elements; how exact they have to be, the bound alone decides.
A program may use at most 64 MiB of HBM per device.

```python
import math
import jax
import jax.numpy as jnp
from jax import lax

WIDTH = 64
ITERS = 8
NS = 4096
NO = 4096


def draw_sim_points(key, part):
    base_key = jax.random.fold_in(key, 0)
    return jax.random.truncated_normal(base_key, -4.0, 4.0, (WIDTH, NS), jnp.float32)


def block_scale(stream_key, dims, cuts, low, high):
    def one(dim, parts):
        steps = jax.random.uniform(jax.random.fold_in(jax.random.fold_in(stream_key, 6), dim), (parts,), jnp.float32, low / len(cuts), high / len(cuts))
        return jnp.repeat(jnp.exp(steps), dims[dim] // parts).reshape((-1,) + (1,) * (len(dims) - dim - 1))

    factor_of = one(*cuts[0])
    for cut in cuts[1:]:
        factor_of = factor_of * one(*cut)
    return factor_of


def normal_values(own_key, dims, width, limit, shards=(), held_as=jnp.bfloat16):
    array = jax.random.normal(own_key, dims, jnp.float32) * width
    if len(shards) > 0:
        array = block_scale(own_key, dims, shards, -0.22, 0.18) * array
    return jnp.clip(array, min=-limit, max=limit).astype(held_as)


def setup_inputs(seed: int = 0) -> dict:
    seeds = jax.random.split(jax.random.key(seed), 5)
    return {
        "sim_points": draw_sim_points(jax.random.fold_in(seeds[4], 71), 0),
        "obs_points": normal_values(seeds[1], (WIDTH, NO), 3.0, 16.0, ((1, 32),), jnp.float32),
        "sim_logw": jnp.clip(jax.random.uniform(seeds[2], (NS,), jnp.float32, -2.5, 2.5) * block_scale(seeds[2], (NS,), ((0, 16),), -0.4, 0.0), -2.5, 2.5),
        "obs_logw": jnp.clip(jax.random.uniform(seeds[3], (NO,), jnp.float32, -2.5, 2.5) * block_scale(seeds[3], (NO,), ((0, 32),), -0.4, 0.0), -2.5, 2.5),
    }


epsilon = 0.05


def pair_cost(points, observed):
    sq_points = jnp.sum(points * points, 0)
    sq_observed = jnp.sum(observed * observed, 0)
    inner_products = lax.dot_general(points, observed, (((0,), (0,)), ((), ())), precision=lax.Precision.HIGHEST, preferred_element_type=jnp.float32)
    return (sq_points[:, None] + sq_observed[None, :] - 2.0 * inner_products) / WIDTH


def reference(sim_points, obs_points, sim_logw, obs_logw):
    log_a = sim_logw - math.log(NS)
    log_b = obs_logw - math.log(NO)
    block_rows = math.gcd(NS, 1024)
    block_count = NS // block_rows
    point_blocks = jnp.transpose(sim_points.reshape(WIDTH, block_count, block_rows), (1, 0, 2))
    weight_blocks = log_a.reshape(block_count, block_rows)

    def row_update(potential_g):
        def one_block(pieces):
            points, weights = pieces
            scores = (potential_g[None, :] - pair_cost(points, obs_points)) / epsilon
            row_top = jnp.max(scores, 1)
            row_mass = jnp.sum(jnp.exp(scores - row_top[:, None]), 1)
            return epsilon * weights - epsilon * (row_top + jnp.log(row_mass))
        return lax.map(one_block, (point_blocks, weight_blocks)).reshape(NS)

    def col_update(potential_f):
        f_blocks = potential_f.reshape(block_count, block_rows)

        def one_block(carry, pieces):
            col_top, col_mass = carry
            points, f_piece = pieces
            scores = (f_piece[:, None] - pair_cost(points, obs_points)) / epsilon
            new_top = jnp.maximum(col_top, jnp.max(scores, 0))
            col_mass = col_mass * jnp.exp(col_top - new_top) + jnp.sum(jnp.exp(scores - new_top[None, :]), 0)
            return (new_top, col_mass), None
        start = (jnp.full((NO,), -jnp.inf, jnp.float32), jnp.zeros((NO,), jnp.float32))
        (col_top, col_mass), unused = lax.scan(one_block, start, (point_blocks, f_blocks))
        return epsilon * log_b - epsilon * (col_top + jnp.log(col_mass))

    potential_g = jnp.zeros((NO,), jnp.float32)
    for iteration in range(ITERS):
        potential_f = row_update(potential_g)
        potential_g = col_update(potential_f)
    f_blocks = potential_f.reshape(block_count, block_rows)

    def block_cost(pieces):
        points, f_piece = pieces
        costs_tile = pair_cost(points, obs_points)
        transport = jnp.exp((f_piece[:, None] + potential_g[None, :] - costs_tile) / epsilon)
        return jnp.sum(transport * costs_tile)
    total_cost = jnp.sum(lax.map(block_cost, (point_blocks, f_blocks)))
    return potential_f, potential_g, jnp.reshape(total_cost, (1,))
```

```python
import functools
import math

import jax
import jax.numpy as jnp
from jax import lax
from jax.experimental import pallas as pl
from jax.experimental.pallas import tpu as pltpu

ITERS = 8
EPSILON = 0.05
LOG2E = 1.0 / math.log(2.0)
PLANE = 4
REBUILD = 3
LIFT = 60.0
MESH = pl.DeviceIdType.MESH
PARTS = 2


def split_rows(row):
    high = row.astype(jnp.bfloat16).astype(jnp.float32)
    rest = row - high
    middle = rest.astype(jnp.bfloat16).astype(jnp.float32)
    low = rest - middle
    shape = (16, row.shape[1])
    index = lax.broadcasted_iota(jnp.int32, shape, 0)
    full = lambda part: jnp.broadcast_to(part, shape)
    rows = jnp.where(
        index == 0,
        full(high),
        jnp.where(index == 1, full(middle), jnp.where(index == 2, full(low), 0.0)),
    )
    return rows.astype(jnp.bfloat16)


def matvec(rows, parts, contract):
    total = None
    for part in parts:
        out = lax.dot_general(
            rows, part[...], (((1,), (contract,)), ((), ())), preferred_element_type=jnp.float32
        )
        total = out if total is None else total + out
    return total[0:1] + total[1:2] + total[2:3]


def to_column(row):
    return jnp.broadcast_to(row, (128, row.shape[1])).T


def to_row(column):
    return jnp.broadcast_to(column, (column.shape[0], 128)).T[0:1]


def body(
    rows_n, cols_n, plane,
    sim_ref, obs_ref, slw_ref, olw_ref,
    f_ref, g_ref, cost_ref,
    simg, obsg, d_ref, k_ref, x_ref,
    row_first, col_first, row_buf, col_buf, end_buf,
    send_sem, recv_sem,
):
    lines = rows_n // plane
    width, n_sim = sim_ref.shape
    n_obs = obs_ref.shape[1]
    n_i = plane * n_sim
    n_j = lines * n_obs
    r = lax.axis_index("row")
    c = lax.axis_index("col")
    z = r // plane
    q = r % plane
    group = plane * cols_n
    me = q * cols_n + c

    plane_peers = []
    for step in range(1, group):
        other = (me + step) % group
        plane_peers.append((z * plane + other // cols_n, other % cols_n))
    line_peers = []
    for step in range(1, lines):
        line_peers.append((((z + step) % lines) * plane + q, c))
    core_peers = []
    for step in range(1, plane):
        core_peers.append((z * plane + (q + step) % plane, c))

    barrier = pltpu.get_barrier_semaphore()
    for peer in plane_peers + line_peers:
        pl.semaphore_signal(barrier, inc=1, device_id=peer, device_id_type=MESH)

    scale = LOG2E / (EPSILON * width)
    x = sim_ref[...]
    y = obs_ref[...]
    pad = simg.shape[1] - width

    def tail(values, n):
        index = lax.broadcasted_iota(jnp.int32, (pad, n), 0)
        out = jnp.zeros((pad, n), jnp.float32)
        for k, value in enumerate(values):
            if value is not None:
                out = jnp.where(index == k, jnp.broadcast_to(value, (pad, n)), out)
        return out

    one = jnp.ones((1, n_sim), jnp.float32)
    simg[q, :width, :] = x
    simg[q, width:, :] = tail(
        [jnp.sum(x * x, 0, keepdims=True), one, slw_ref[...]], n_sim
    )
    ones_obs = jnp.full((1, n_obs), scale, jnp.float32)
    obsg[z, :width, :] = y * (-2.0 * scale)
    obsg[z, width:, :] = tail(
        [ones_obs, jnp.sum(y * y, 0, keepdims=True) * scale, None, olw_ref[...]], n_obs
    )
    pl.semaphore_wait(barrier, len(plane_peers) + len(line_peers))

    def exchange(buf, own, peers, sem):
        for peer in peers:
            pltpu.make_async_remote_copy(
                src_ref=buf.at[own], dst_ref=buf.at[own],
                send_sem=send_sem.at[sem], recv_sem=recv_sem.at[sem],
                device_id=peer, device_id_type=MESH,
            ).start()

    def finish(buf, peers, sem):
        if peers:
            some = buf.at[pl.ds(0, len(peers))]
            pltpu.make_async_copy(some, some, recv_sem.at[sem]).wait()
            pltpu.make_async_copy(some, some, send_sem.at[sem]).wait()

    exchange(obsg, z, line_peers, 0)
    exchange(simg, q, core_peers, 1)
    finish(obsg, line_peers, 0)
    finish(simg, core_peers, 1)

    log_a = jnp.concatenate(
        [simg[k, width + 2:width + 3, :] for k in range(plane)], axis=1
    ) * LOG2E - math.log2(n_sim * rows_n)
    log_b = jnp.concatenate(
        [obsg[k, width + 3:width + 4, :] for k in range(lines)], axis=1
    ) * LOG2E - math.log2(n_obs * rows_n * cols_n)

    for k in range(lines):
        left = obsg[k].T
        for m in range(plane):
            d_ref[k * n_obs:(k + 1) * n_obs, m * n_sim:(m + 1) * n_sim] = lax.dot_general(
                left, simg[m], (((1,), (0,)), ((), ())),
                precision=lax.Precision.HIGHEST, preferred_element_type=jnp.float32,
            )

    d = d_ref[...]
    low = jnp.min(d, 0, keepdims=True)
    mass = jnp.sum(jnp.exp2(low - d), 0, keepdims=True)
    row_first[me, 0:1, :] = low
    row_first[me, 1:2, :] = mass
    exchange(row_first, me, plane_peers, 2)
    finish(row_first, plane_peers, 2)

    def merge(buf, count):
        low = buf[0, 0:1, :]
        for k in range(1, count):
            low = jnp.minimum(low, buf[k, 0:1, :])
        mass = buf[0, 1:2, :] * jnp.exp2(low - buf[0, 0:1, :])
        for k in range(1, count):
            mass = mass + buf[k, 1:2, :] * jnp.exp2(low - buf[k, 0:1, :])
        return low - jnp.log2(mass)

    f = log_a + merge(row_first, group)
    scores = d_ref[...] - f
    low = jnp.min(scores, 1, keepdims=True)
    mass = jnp.sum(jnp.exp2(low - scores), 1, keepdims=True)
    col_first[z, 0:1, :] = to_row(low)
    col_first[z, 1:2, :] = to_row(mass)
    exchange(col_first, z, line_peers, 3)
    finish(col_first, line_peers, 3)
    g = log_b + merge(col_first, lines)

    a_lifted = jnp.exp2(log_a + LIFT)
    b_lifted = jnp.exp2(log_b + LIFT)

    def store_parts(ref, value, rows):
        high = value.astype(jnp.bfloat16)
        ref[0, rows, :] = high
        if PARTS > 1:
            ref[1, rows, :] = (value - high.astype(jnp.float32)).astype(jnp.bfloat16)

    def build(f, g, with_cost):
        column = to_column(g + LIFT)
        for j in range(0, n_j, 64):
            rows = pl.ds(j, 64)
            piece = column[j:j + 64]
            shift = jnp.concatenate([piece] * (n_i // 128), axis=1)
            values = jnp.exp2((f + shift) - d_ref[rows, :])
            store_parts(k_ref, values, rows)
            if with_cost:
                store_parts(x_ref, values * d_ref[rows, :], rows)

    def total_of(buf, count):
        total = buf[0, 0:1, :]
        for k in range(1, count):
            total = total + buf[k, 0:1, :]
        return total

    def row_half(v_rows, parity):
        buf = row_buf.at[parity]
        buf[me, 0:1, :] = matvec(v_rows, [k_ref.at[p] for p in range(PARTS)], 0)
        exchange(buf, me, plane_peers, 4 + parity)
        finish(buf, plane_peers, 4 + parity)
        return a_lifted / total_of(buf, group)

    def col_half(u, parity):
        buf = col_buf.at[parity]
        buf[z, 0:1, :] = matvec(split_rows(u), [k_ref.at[p] for p in range(PARTS)], 1)
        exchange(buf, z, line_peers, 6 + parity)
        finish(buf, line_peers, 6 + parity)
        return b_lifted / total_of(buf, lines)

    done = 1
    while done < ITERS - 1:
        count = min(REBUILD, ITERS - 1 - done)
        build(f, g, False)

        def step(iteration, carry):
            _, v = carry
            parity = iteration % 2
            u = row_half(split_rows(v), parity)
            return u, col_half(u, parity)

        u, v = lax.fori_loop(
            done, done + count, step,
            (jnp.ones((1, n_i), jnp.float32), jnp.ones((1, n_j), jnp.float32)),
        )
        f = f + jnp.log2(u)
        g = g + jnp.log2(v)
        done += count

    build(f, g, True)
    parity = (ITERS - 1) % 2
    u = row_half(split_rows(jnp.ones((1, n_j), jnp.float32)), parity)
    u_rows = split_rows(u)
    col_first[z, 0:1, :] = matvec(u_rows, [k_ref.at[p] for p in range(PARTS)], 1)
    col_first[z, 1:2, :] = matvec(u_rows, [x_ref.at[p] for p in range(PARTS)], 1)
    exchange(col_first, z, line_peers, 3)
    f = f + jnp.log2(u)
    f_mine = f[:, 0:n_sim]
    for k in range(1, plane):
        f_mine = jnp.where(q == k, f[:, k * n_sim:(k + 1) * n_sim], f_mine)
    f_ref[...] = f_mine * (EPSILON / LOG2E)
    finish(col_first, line_peers, 3)
    sums = col_first[0]
    for k in range(1, lines):
        sums = sums + col_first[k]
    v = b_lifted / sums[0:1]
    share = jnp.sum(v * 2.0 ** -LIFT * sums[1:2], axis=1, keepdims=True)
    end_buf[me] = jnp.broadcast_to(share * (EPSILON / LOG2E), (1, 128))
    exchange(end_buf, me, plane_peers, 8)
    g = g + jnp.log2(v)
    g_mine = g[:, 0:n_obs]
    for k in range(1, lines):
        g_mine = jnp.where(z == k, g[:, k * n_obs:(k + 1) * n_obs], g_mine)
    g_ref[...] = g_mine * (EPSILON / LOG2E)
    finish(end_buf, plane_peers, 8)
    cost_ref[...] = total_of(end_buf, group)[:, 0:1]


def on_device(sizes, sim_points, obs_points, sim_logw, obs_logw):
    rows_n, cols_n = sizes
    plane = math.gcd(PLANE, rows_n)
    lines = rows_n // plane
    group = plane * cols_n
    width, n_sim = sim_points.shape
    n_obs = obs_points.shape[1]
    n_i, n_j = plane * n_sim, lines * n_obs
    f32, bf16 = jnp.float32, jnp.bfloat16
    depth = -(-width // 8) * 8 + 8
    assert width % 8 == 0
    vmem = pl.BlockSpec(memory_space=pltpu.VMEM)
    f, g, cost = pl.pallas_call(
        functools.partial(body, rows_n, cols_n, plane),
        out_shape=(
            jax.ShapeDtypeStruct((1, n_sim), f32),
            jax.ShapeDtypeStruct((1, n_obs), f32),
            jax.ShapeDtypeStruct((1, 1), f32),
        ),
        in_specs=[vmem] * 4,
        out_specs=(vmem,) * 3,
        scratch_shapes=[
            pltpu.VMEM((plane, depth, n_sim), f32),
            pltpu.VMEM((lines, depth, n_obs), f32),
            pltpu.VMEM((n_j, n_i), f32),
            pltpu.VMEM((PARTS, n_j, n_i), bf16),
            pltpu.VMEM((PARTS, n_j, n_i), bf16),
            pltpu.VMEM((group, 2, n_i), f32),
            pltpu.VMEM((lines, 2, n_j), f32),
            pltpu.VMEM((2, group, 1, n_i), f32),
            pltpu.VMEM((2, lines, 1, n_j), f32),
            pltpu.VMEM((group, 1, 128), f32),
            pltpu.SemaphoreType.DMA((9,)),
            pltpu.SemaphoreType.DMA((9,)),
        ],
        compiler_params=pltpu.CompilerParams(
            collective_id=0, has_side_effects=True, vmem_limit_bytes=48 * 2**20
        ),
        name="sinkhorn",
    )(sim_points, obs_points, sim_logw[None, :], obs_logw[None, :])
    return f[0], g[0], cost[0]


def solution(mesh):
    P = jax.sharding.PartitionSpec
    in_specs = (P(None, "row"), P(None, ("row", "col")), P("row"), P(("row", "col")))
    out_specs = (P("row"), P(("row", "col")), P())
    sizes = (mesh.shape["row"], mesh.shape["col"])
    return jax.shard_map(
        functools.partial(on_device, sizes),
        mesh=mesh, in_specs=in_specs, out_specs=out_specs, check_vma=False,
    )
```

```python
import functools
import math

import jax
import jax.numpy as jnp
from jax import lax
from jax.experimental import pallas as pl
from jax.experimental.pallas import tpu as pltpu

ITERS = 8
EPSILON = 0.05
LOG2E = 1.0 / math.log(2.0)
PLANE = 4
REBUILD = 3
LIFT = 60.0
MESH = pl.DeviceIdType.MESH
PARTS = 2


def split_rows(row):
    high = row.astype(jnp.bfloat16).astype(jnp.float32)
    rest = row - high
    middle = rest.astype(jnp.bfloat16).astype(jnp.float32)
    low = rest - middle
    shape = (16, row.shape[1])
    index = lax.broadcasted_iota(jnp.int32, shape, 0)
    full = lambda part: jnp.broadcast_to(part, shape)
    rows = jnp.where(
        index == 0,
        full(high),
        jnp.where(index == 1, full(middle), jnp.where(index == 2, full(low), 0.0)),
    )
    return rows.astype(jnp.bfloat16)


def matvec(rows, parts, contract):
    total = None
    for part in parts:
        out = lax.dot_general(
            rows, part[...], (((1,), (contract,)), ((), ())), preferred_element_type=jnp.float32
        )
        total = out if total is None else total + out
    return total[0:1] + total[1:2] + total[2:3]


def to_column(row):
    return jnp.broadcast_to(row, (128, row.shape[1])).T


def to_row(column):
    return jnp.broadcast_to(column, (column.shape[0], 128)).T[0:1]


def body(
    rows_n, cols_n, plane,
    sim_ref, obs_ref, slw_ref, olw_ref,
    out_ref,
    slw_buf, olw_buf, load_sem, simg, obsg, d_ref, k_ref, x_ref,
    row_first, col_first, row_buf, col_buf, end_buf,
    send_sem, recv_sem,
):
    lines = rows_n // plane
    width, n_sim = sim_ref.shape
    n_obs = obs_ref.shape[1]
    n_i = plane * n_sim
    n_j = lines * n_obs
    r = lax.axis_index("row")
    c = lax.axis_index("col")
    z = r // plane
    q = r % plane
    group = plane * cols_n
    me = q * cols_n + c

    plane_peers = []
    for step in range(1, group):
        other = (me + step) % group
        plane_peers.append((z * plane + other // cols_n, other % cols_n))
    line_peers = []
    for step in range(1, lines):
        line_peers.append((((z + step) % lines) * plane + q, c))
    core_peers = []
    for step in range(1, plane):
        core_peers.append((z * plane + (q + step) % plane, c))

    loads = [
        pltpu.make_async_copy(sim_ref, simg.at[q, pl.ds(0, width)], load_sem.at[0]),
        pltpu.make_async_copy(obs_ref, obsg.at[z, pl.ds(0, width)], load_sem.at[1]),
        pltpu.make_async_copy(slw_ref, slw_buf, load_sem.at[2]),
        pltpu.make_async_copy(olw_ref, olw_buf, load_sem.at[3]),
    ]
    for load in loads:
        load.start()
    barrier = pltpu.get_barrier_semaphore()
    for peer in plane_peers + line_peers:
        pl.semaphore_signal(barrier, inc=1, device_id=peer, device_id_type=MESH)

    scale = LOG2E / (EPSILON * width)
    for load in loads:
        load.wait()
    x = simg[q, :width, :]
    y = obsg[z, :width, :]
    pad = simg.shape[1] - width

    def tail(values, n):
        index = lax.broadcasted_iota(jnp.int32, (pad, n), 0)
        out = jnp.zeros((pad, n), jnp.float32)
        for k, value in enumerate(values):
            if value is not None:
                out = jnp.where(index == k, jnp.broadcast_to(value, (pad, n)), out)
        return out

    one = jnp.ones((1, n_sim), jnp.float32)
    simg[q, width:, :] = tail(
        [jnp.sum(x * x, 0, keepdims=True), one, slw_buf[...]], n_sim
    )
    ones_obs = jnp.ones((1, n_obs), jnp.float32)
    obsg[z, width:, :] = tail(
        [ones_obs, jnp.sum(y * y, 0, keepdims=True), None, olw_buf[...]], n_obs
    )
    pl.semaphore_wait(barrier, len(plane_peers) + len(line_peers))

    def exchange(buf, own, peers, sem):
        for peer in peers:
            pltpu.make_async_remote_copy(
                src_ref=buf.at[own], dst_ref=buf.at[own],
                send_sem=send_sem.at[sem], recv_sem=recv_sem.at[sem],
                device_id=peer, device_id_type=MESH,
            ).start()

    def finish(buf, peers, sem):
        if peers:
            some = buf.at[pl.ds(0, len(peers))]
            pltpu.make_async_copy(some, some, recv_sem.at[sem]).wait()
            pltpu.make_async_copy(some, some, send_sem.at[sem]).wait()

    exchange(obsg, z, line_peers, 0)
    exchange(simg, q, core_peers, 1)
    finish(obsg, line_peers, 0)
    finish(simg, core_peers, 1)

    log_a = jnp.concatenate(
        [simg[k, width + 2:width + 3, :] for k in range(plane)], axis=1
    ) * LOG2E - math.log2(n_sim * rows_n)
    log_b = jnp.concatenate(
        [obsg[k, width + 3:width + 4, :] for k in range(lines)], axis=1
    ) * LOG2E - math.log2(n_obs * rows_n * cols_n)

    index = lax.broadcasted_iota(jnp.int32, (width + pad, n_obs), 0)
    factor = jnp.where(index < width, -2.0 * scale, scale)
    for k in range(lines):
        left = (obsg[k] * factor).T
        for m in range(plane):
            d_ref[k * n_obs:(k + 1) * n_obs, m * n_sim:(m + 1) * n_sim] = lax.dot_general(
                left, simg[m], (((1,), (0,)), ((), ())),
                precision=lax.Precision.HIGHEST, preferred_element_type=jnp.float32,
            )

    d = d_ref[...]
    low = jnp.min(d, 0, keepdims=True)
    mass = jnp.sum(jnp.exp2(low - d), 0, keepdims=True)
    row_first[me, 0:1, :] = low
    row_first[me, 1:2, :] = mass
    exchange(row_first, me, plane_peers, 2)
    finish(row_first, plane_peers, 2)

    def merge(buf, count):
        low = buf[0, 0:1, :]
        for k in range(1, count):
            low = jnp.minimum(low, buf[k, 0:1, :])
        mass = buf[0, 1:2, :] * jnp.exp2(low - buf[0, 0:1, :])
        for k in range(1, count):
            mass = mass + buf[k, 1:2, :] * jnp.exp2(low - buf[k, 0:1, :])
        return low - jnp.log2(mass)

    f = log_a + merge(row_first, group)
    scores = d_ref[...] - f
    low = jnp.min(scores, 1, keepdims=True)
    mass = jnp.sum(jnp.exp2(low - scores), 1, keepdims=True)
    col_first[z, 0:1, :] = to_row(low)
    col_first[z, 1:2, :] = to_row(mass)
    exchange(col_first, z, line_peers, 3)
    finish(col_first, line_peers, 3)
    g = log_b + merge(col_first, lines)

    a_lifted = jnp.exp2(log_a + LIFT)
    b_lifted = jnp.exp2(log_b + LIFT)

    def store_parts(ref, value, rows, parts):
        high = value.astype(jnp.bfloat16)
        ref[0, rows, :] = high
        if parts > 1:
            ref[1, rows, :] = (value - high.astype(jnp.float32)).astype(jnp.bfloat16)

    def build(f, g, last):
        parts = PARTS if last else 1
        column = to_column(g + LIFT)
        for j in range(0, n_j, 64):
            rows = pl.ds(j, 64)
            piece = column[j:j + 64]
            shift = jnp.concatenate([piece] * (n_i // 128), axis=1)
            values = jnp.exp2((f + shift) - d_ref[rows, :])
            store_parts(k_ref, values, rows, parts)
            if last:
                store_parts(x_ref, values * d_ref[rows, :], rows, 1)

    def total_of(buf, count):
        total = buf[0, 0:1, :]
        for k in range(1, count):
            total = total + buf[k, 0:1, :]
        return total

    def row_half(v_rows, parity, parts):
        buf = row_buf.at[parity]
        buf[me, 0:1, :] = matvec(v_rows, [k_ref.at[p] for p in range(parts)], 0)
        exchange(buf, me, plane_peers, 4 + parity)
        finish(buf, plane_peers, 4 + parity)
        return a_lifted / total_of(buf, group)

    def col_half(u, parity):
        buf = col_buf.at[parity]
        buf[z, 0:1, :] = matvec(split_rows(u), [k_ref.at[0]], 1)
        exchange(buf, z, line_peers, 6 + parity)
        finish(buf, line_peers, 6 + parity)
        return b_lifted / total_of(buf, lines)

    done = 1
    while done < ITERS - 1:
        count = min(REBUILD, ITERS - 1 - done)
        build(f, g, False)

        def step(iteration, carry):
            _, v = carry
            parity = iteration % 2
            u = row_half(split_rows(v), parity, 1)
            return u, col_half(u, parity)

        u, v = lax.fori_loop(
            done, done + count, step,
            (jnp.ones((1, n_i), jnp.float32), jnp.ones((1, n_j), jnp.float32)),
        )
        f = f + jnp.log2(u)
        g = g + jnp.log2(v)
        done += count

    build(f, g, True)
    parity = (ITERS - 1) % 2
    u = row_half(split_rows(jnp.ones((1, n_j), jnp.float32)), parity, PARTS)
    u_rows = split_rows(u)
    col_first[z, 0:1, :] = matvec(u_rows, [k_ref.at[p] for p in range(PARTS)], 1)
    col_first[z, 1:2, :] = matvec(u_rows, [x_ref.at[0]], 1)
    exchange(col_first, z, line_peers, 3)
    f = f + jnp.log2(u)
    f_mine = f[:, 0:n_sim]
    for k in range(1, plane):
        f_mine = jnp.where(q == k, f[:, k * n_sim:(k + 1) * n_sim], f_mine)
    out_ref[:, 0:n_sim] = f_mine * (EPSILON / LOG2E)
    finish(col_first, line_peers, 3)
    sums = col_first[0]
    for k in range(1, lines):
        sums = sums + col_first[k]
    v = b_lifted / sums[0:1]
    share = jnp.sum(v * 2.0 ** -LIFT * sums[1:2], axis=1, keepdims=True)
    end_buf[me] = jnp.broadcast_to(share * (EPSILON / LOG2E), (1, 128))
    exchange(end_buf, me, plane_peers, 8)
    g = g + jnp.log2(v)
    g_mine = g[:, 0:n_obs]
    for k in range(1, lines):
        g_mine = jnp.where(z == k, g[:, k * n_obs:(k + 1) * n_obs], g_mine)
    out_ref[:, n_sim:n_sim + n_obs] = g_mine * (EPSILON / LOG2E)
    finish(end_buf, plane_peers, 8)
    out_ref[:, n_sim + n_obs:] = total_of(end_buf, group)


def on_device(sizes, sim_points, obs_points, sim_logw, obs_logw):
    rows_n, cols_n = sizes
    plane = math.gcd(PLANE, rows_n)
    lines = rows_n // plane
    group = plane * cols_n
    width, n_sim = sim_points.shape
    n_obs = obs_points.shape[1]
    n_i, n_j = plane * n_sim, lines * n_obs
    f32, bf16 = jnp.float32, jnp.bfloat16
    depth = -(-width // 8) * 8 + 8
    assert width % 8 == 0
    vmem = pl.BlockSpec(memory_space=pltpu.VMEM)
    out = pl.pallas_call(
        functools.partial(body, rows_n, cols_n, plane),
        out_shape=jax.ShapeDtypeStruct((1, n_sim + n_obs + 128), f32),
        in_specs=[pl.BlockSpec(memory_space=pltpu.HBM)] * 4,
        out_specs=vmem,
        scratch_shapes=[
            pltpu.VMEM((1, n_sim), f32),
            pltpu.VMEM((1, n_obs), f32),
            pltpu.SemaphoreType.DMA((4,)),
            pltpu.VMEM((plane, depth, n_sim), f32),
            pltpu.VMEM((lines, depth, n_obs), f32),
            pltpu.VMEM((n_j, n_i), f32),
            pltpu.VMEM((PARTS, n_j, n_i), bf16),
            pltpu.VMEM((1, n_j, n_i), bf16),
            pltpu.VMEM((group, 2, n_i), f32),
            pltpu.VMEM((lines, 2, n_j), f32),
            pltpu.VMEM((2, group, 1, n_i), f32),
            pltpu.VMEM((2, lines, 1, n_j), f32),
            pltpu.VMEM((group, 1, 128), f32),
            pltpu.SemaphoreType.DMA((9,)),
            pltpu.SemaphoreType.DMA((9,)),
        ],
        compiler_params=pltpu.CompilerParams(
            collective_id=0, has_side_effects=True, vmem_limit_bytes=57 * 2**20
        ),
        name="sinkhorn",
    )(sim_points, obs_points, sim_logw[None, :], obs_logw[None, :])
    out = out[0]
    return out[:n_sim], out[n_sim:n_sim + n_obs], out[n_sim + n_obs:n_sim + n_obs + 1]


def solution(mesh):
    P = jax.sharding.PartitionSpec
    in_specs = (P(None, "row"), P(None, ("row", "col")), P("row"), P(("row", "col")))
    out_specs = (P("row"), P(("row", "col")), P())
    sizes = (mesh.shape["row"], mesh.shape["col"])
    return jax.shard_map(
        functools.partial(on_device, sizes),
        mesh=mesh, in_specs=in_specs, out_specs=out_specs, check_vma=False,
    )
```

```python
import functools
import math

import jax
import jax.numpy as jnp
from jax import lax
from jax.experimental import pallas as pl
from jax.experimental.pallas import tpu as pltpu

ITERS = 8
EPSILON = 0.05
LOG2E = 1.0 / math.log(2.0)
PLANE = 4
REBUILD = 2
LIFT = 60.0
MESH = pl.DeviceIdType.MESH
PARTS = 2


def split_rows(row):
    high = row.astype(jnp.bfloat16).astype(jnp.float32)
    rest = row - high
    middle = rest.astype(jnp.bfloat16).astype(jnp.float32)
    low = rest - middle
    shape = (16, row.shape[1])
    index = lax.broadcasted_iota(jnp.int32, shape, 0)
    full = lambda part: jnp.broadcast_to(part, shape)
    rows = jnp.where(
        index == 0,
        full(high),
        jnp.where(index == 1, full(middle), jnp.where(index == 2, full(low), 0.0)),
    )
    return rows.astype(jnp.bfloat16)


def matvec(rows, parts, contract):
    total = None
    for part in parts:
        out = lax.dot_general(
            rows, part[...], (((1,), (contract,)), ((), ())), preferred_element_type=jnp.float32
        )
        total = out if total is None else total + out
    return total[0:1] + total[1:2] + total[2:3]


def to_column(row):
    return jnp.broadcast_to(row, (128, row.shape[1])).T


def to_row(column):
    return jnp.broadcast_to(column, (column.shape[0], 128)).T[0:1]


def body(
    rows_n, cols_n, plane,
    sim_ref, obs_ref, slw_ref, olw_ref,
    out_ref,
    slw_buf, olw_buf, load_sem, simg, obsg, d_ref, k_ref, x_ref,
    row_first, col_first, row_buf, col_buf, end_buf,
    send_sem, recv_sem,
):
    lines = rows_n // plane
    width, n_sim = sim_ref.shape
    n_obs = obs_ref.shape[1]
    n_i = plane * n_sim
    n_j = lines * n_obs
    r = lax.axis_index("row")
    c = lax.axis_index("col")
    z = r // plane
    q = r % plane
    group = plane * cols_n
    me = q * cols_n + c

    plane_peers = []
    for step in range(1, group):
        other = (me + step) % group
        plane_peers.append((z * plane + other // cols_n, other % cols_n))
    line_peers = []
    for step in range(1, lines):
        line_peers.append((((z + step) % lines) * plane + q, c))
    core_peers = []
    for step in range(1, plane):
        core_peers.append((z * plane + (q + step) % plane, c))

    loads = [
        pltpu.make_async_copy(sim_ref, simg.at[q, pl.ds(0, width)], load_sem.at[0]),
        pltpu.make_async_copy(obs_ref, obsg.at[z, pl.ds(0, width)], load_sem.at[1]),
        pltpu.make_async_copy(slw_ref, slw_buf, load_sem.at[2]),
        pltpu.make_async_copy(olw_ref, olw_buf, load_sem.at[3]),
    ]
    for load in loads:
        load.start()
    barrier = pltpu.get_barrier_semaphore()
    for peer in plane_peers + line_peers:
        pl.semaphore_signal(barrier, inc=1, device_id=peer, device_id_type=MESH)

    scale = LOG2E / (EPSILON * width)
    for load in loads:
        load.wait()
    x = simg[q, :width, :]
    y = obsg[z, :width, :]
    pad = simg.shape[1] - width

    def tail(values, n):
        index = lax.broadcasted_iota(jnp.int32, (pad, n), 0)
        out = jnp.zeros((pad, n), jnp.float32)
        for k, value in enumerate(values):
            if value is not None:
                out = jnp.where(index == k, jnp.broadcast_to(value, (pad, n)), out)
        return out

    one = jnp.ones((1, n_sim), jnp.float32)
    simg[q, width:, :] = tail(
        [jnp.sum(x * x, 0, keepdims=True), one, slw_buf[...]], n_sim
    )
    ones_obs = jnp.ones((1, n_obs), jnp.float32)
    obsg[z, width:, :] = tail(
        [ones_obs, jnp.sum(y * y, 0, keepdims=True), None, olw_buf[...]], n_obs
    )
    pl.semaphore_wait(barrier, len(plane_peers) + len(line_peers))

    def exchange(buf, own, peers, sem):
        for peer in peers:
            pltpu.make_async_remote_copy(
                src_ref=buf.at[own], dst_ref=buf.at[own],
                send_sem=send_sem.at[sem], recv_sem=recv_sem.at[sem],
                device_id=peer, device_id_type=MESH,
            ).start()

    def finish(buf, peers, sem):
        if peers:
            some = buf.at[pl.ds(0, len(peers))]
            pltpu.make_async_copy(some, some, recv_sem.at[sem]).wait()
            pltpu.make_async_copy(some, some, send_sem.at[sem]).wait()

    exchange(obsg, z, line_peers, 0)
    exchange(simg, q, core_peers, 1)
    finish(obsg, line_peers, 0)
    index = lax.broadcasted_iota(jnp.int32, (width + pad, n_obs), 0)
    factor = jnp.where(index < width, -2.0 * scale, scale)
    lefts = [(obsg[k] * factor).T for k in range(lines)]
    finish(simg, core_peers, 1)

    log_a = jnp.concatenate(
        [simg[k, width + 2:width + 3, :] for k in range(plane)], axis=1
    ) * LOG2E - math.log2(n_sim * rows_n)
    log_b = jnp.concatenate(
        [obsg[k, width + 3:width + 4, :] for k in range(lines)], axis=1
    ) * LOG2E - math.log2(n_obs * rows_n * cols_n)

    for k in range(lines):
        left = lefts[k]
        for m in range(plane):
            d_ref[k * n_obs:(k + 1) * n_obs, m * n_sim:(m + 1) * n_sim] = lax.dot_general(
                left, simg[m], (((1,), (0,)), ((), ())),
                precision=lax.Precision.HIGHEST, preferred_element_type=jnp.float32,
            )

    d = d_ref[...]
    low = jnp.min(d, 0, keepdims=True)
    mass = jnp.sum(jnp.exp2(low - d), 0, keepdims=True)
    row_first[me, 0:1, :] = low
    row_first[me, 1:2, :] = mass
    exchange(row_first, me, plane_peers, 2)
    finish(row_first, plane_peers, 2)

    def merge(buf, count):
        low = buf[0, 0:1, :]
        for k in range(1, count):
            low = jnp.minimum(low, buf[k, 0:1, :])
        mass = buf[0, 1:2, :] * jnp.exp2(low - buf[0, 0:1, :])
        for k in range(1, count):
            mass = mass + buf[k, 1:2, :] * jnp.exp2(low - buf[k, 0:1, :])
        return low - jnp.log2(mass)

    f = log_a + merge(row_first, group)
    scores = d_ref[...] - f
    low = jnp.min(scores, 1, keepdims=True)
    mass = jnp.sum(jnp.exp2(low - scores), 1, keepdims=True)
    col_first[z, 0:1, :] = to_row(low)
    col_first[z, 1:2, :] = to_row(mass)
    exchange(col_first, z, line_peers, 3)
    finish(col_first, line_peers, 3)
    g = log_b + merge(col_first, lines)

    a_lifted = jnp.exp2(log_a + LIFT)
    b_lifted = jnp.exp2(log_b + LIFT)

    def store_parts(ref, value, rows, parts):
        high = value.astype(jnp.bfloat16)
        ref[0, rows, :] = high
        if parts > 1:
            ref[1, rows, :] = (value - high.astype(jnp.float32)).astype(jnp.bfloat16)

    def build(f, g, last):
        parts = PARTS if last else 1
        column = to_column(g + LIFT)
        for j in range(0, n_j, 64):
            rows = pl.ds(j, 64)
            piece = column[j:j + 64]
            shift = jnp.concatenate([piece] * (n_i // 128), axis=1)
            values = jnp.exp2((f + shift) - d_ref[rows, :])
            store_parts(k_ref, values, rows, parts)
            if last:
                store_parts(x_ref, values * d_ref[rows, :], rows, 1)

    def total_of(buf, count):
        total = buf[0, 0:1, :]
        for k in range(1, count):
            total = total + buf[k, 0:1, :]
        return total

    def row_half(v_rows, parity, parts):
        buf = row_buf.at[parity]
        buf[me, 0:1, :] = matvec(v_rows, [k_ref.at[p] for p in range(parts)], 0)
        exchange(buf, me, plane_peers, 4 + parity)
        finish(buf, plane_peers, 4 + parity)
        return a_lifted / total_of(buf, group)

    def col_start(u, parity):
        buf = col_buf.at[parity]
        buf[z, 0:1, :] = matvec(split_rows(u), [k_ref.at[0]], 1)
        exchange(buf, z, line_peers, 6 + parity)

    def col_finish(parity):
        buf = col_buf.at[parity]
        finish(buf, line_peers, 6 + parity)
        return b_lifted / total_of(buf, lines)

    def block(first, f, g, v, last):
        for k in range(REBUILD):
            parity = (first + k) % 2
            u = row_half(split_rows(v), parity, 1)
            col_start(u, parity)
            if k < REBUILD - 1:
                v = col_finish(parity)
        f = f + jnp.log2(u)
        g = g + jnp.log2(v)
        build(f, g, last)
        return f, g, col_finish(parity) / v

    blocks = (ITERS - 2) // REBUILD
    assert blocks * REBUILD == ITERS - 2 and REBUILD % 2 == 0
    build(f, g, False)
    f, g, v = lax.fori_loop(
        0, blocks - 1, lambda k, carry: block(1, *carry, False),
        (f, g, jnp.ones((1, n_j), jnp.float32)),
    )
    f, g, v = block(1, f, g, v, True)

    u = row_half(split_rows(v), (ITERS - 1) % 2, PARTS)
    u_rows = split_rows(u)
    col_first[z, 0:1, :] = matvec(u_rows, [k_ref.at[p] for p in range(PARTS)], 1)
    col_first[z, 1:2, :] = matvec(u_rows, [x_ref.at[0]], 1)
    exchange(col_first, z, line_peers, 3)
    f = f + jnp.log2(u)
    f_mine = f[:, 0:n_sim]
    for k in range(1, plane):
        f_mine = jnp.where(q == k, f[:, k * n_sim:(k + 1) * n_sim], f_mine)
    out_ref[:, 0:n_sim] = f_mine * (EPSILON / LOG2E)
    finish(col_first, line_peers, 3)
    sums = col_first[0]
    for k in range(1, lines):
        sums = sums + col_first[k]
    v = b_lifted / sums[0:1]
    share = jnp.sum(v * 2.0 ** -LIFT * sums[1:2], axis=1, keepdims=True)
    end_buf[me] = jnp.broadcast_to(share * (EPSILON / LOG2E), (1, 128))
    exchange(end_buf, me, plane_peers, 8)
    g = g + jnp.log2(v)
    g_mine = g[:, 0:n_obs]
    for k in range(1, lines):
        g_mine = jnp.where(z == k, g[:, k * n_obs:(k + 1) * n_obs], g_mine)
    out_ref[:, n_sim:n_sim + n_obs] = g_mine * (EPSILON / LOG2E)
    finish(end_buf, plane_peers, 8)
    out_ref[:, n_sim + n_obs:] = total_of(end_buf, group)


def on_device(sizes, sim_points, obs_points, sim_logw, obs_logw):
    rows_n, cols_n = sizes
    plane = math.gcd(PLANE, rows_n)
    lines = rows_n // plane
    group = plane * cols_n
    width, n_sim = sim_points.shape
    n_obs = obs_points.shape[1]
    n_i, n_j = plane * n_sim, lines * n_obs
    f32, bf16 = jnp.float32, jnp.bfloat16
    depth = -(-width // 8) * 8 + 8
    assert width % 8 == 0
    vmem = pl.BlockSpec(memory_space=pltpu.VMEM)
    out = pl.pallas_call(
        functools.partial(body, rows_n, cols_n, plane),
        out_shape=jax.ShapeDtypeStruct((1, n_sim + n_obs + 128), f32),
        in_specs=[pl.BlockSpec(memory_space=pltpu.HBM)] * 4,
        out_specs=vmem,
        scratch_shapes=[
            pltpu.VMEM((1, n_sim), f32),
            pltpu.VMEM((1, n_obs), f32),
            pltpu.SemaphoreType.DMA((4,)),
            pltpu.VMEM((plane, depth, n_sim), f32),
            pltpu.VMEM((lines, depth, n_obs), f32),
            pltpu.VMEM((n_j, n_i), f32),
            pltpu.VMEM((PARTS, n_j, n_i), bf16),
            pltpu.VMEM((1, n_j, n_i), bf16),
            pltpu.VMEM((group, 2, n_i), f32),
            pltpu.VMEM((lines, 2, n_j), f32),
            pltpu.VMEM((2, group, 1, n_i), f32),
            pltpu.VMEM((2, lines, 1, n_j), f32),
            pltpu.VMEM((group, 1, 128), f32),
            pltpu.SemaphoreType.DMA((9,)),
            pltpu.SemaphoreType.DMA((9,)),
        ],
        compiler_params=pltpu.CompilerParams(
            collective_id=0, has_side_effects=True, vmem_limit_bytes=57 * 2**20
        ),
        name="sinkhorn",
    )(sim_points, obs_points, sim_logw[None, :], obs_logw[None, :])
    out = out[0]
    return out[:n_sim], out[n_sim:n_sim + n_obs], out[n_sim + n_obs:n_sim + n_obs + 1]


def solution(mesh):
    P = jax.sharding.PartitionSpec
    in_specs = (P(None, "row"), P(None, ("row", "col")), P("row"), P(("row", "col")))
    out_specs = (P("row"), P(("row", "col")), P())
    sizes = (mesh.shape["row"], mesh.shape["col"])
    return jax.shard_map(
        functools.partial(on_device, sizes),
        mesh=mesh, in_specs=in_specs, out_specs=out_specs, check_vma=False,
    )
```

```python
import functools
import math

import jax
import jax.numpy as jnp
from jax import lax
from jax.experimental import pallas as pl
from jax.experimental.pallas import tpu as pltpu

ITERS = 8
EPSILON = 0.05
LOG2E = 1.0 / math.log(2.0)
PLANE = 4
REBUILD = 2
LIFT = 60.0
MESH = pl.DeviceIdType.MESH
PARTS = 2


def split_rows(row):
    high = row.astype(jnp.bfloat16).astype(jnp.float32)
    rest = row - high
    middle = rest.astype(jnp.bfloat16).astype(jnp.float32)
    low = rest - middle
    shape = (16, row.shape[1])
    index = lax.broadcasted_iota(jnp.int32, shape, 0)
    full = lambda part: jnp.broadcast_to(part, shape)
    rows = jnp.where(
        index == 0,
        full(high),
        jnp.where(index == 1, full(middle), jnp.where(index == 2, full(low), 0.0)),
    )
    return rows.astype(jnp.bfloat16)


def matvec(rows, parts, contract):
    total = None
    for part in parts:
        out = lax.dot_general(
            rows, part[...], (((1,), (contract,)), ((), ())), preferred_element_type=jnp.float32
        )
        total = out if total is None else total + out
    return total[0:1] + total[1:2] + total[2:3]


def to_column(row):
    return jnp.broadcast_to(row, (128, row.shape[1])).T


def to_row(column):
    return jnp.broadcast_to(column, (column.shape[0], 128)).T[0:1]


def body(
    rows_n, cols_n, plane,
    sim_ref, obs_ref, slw_ref, olw_ref,
    out_ref,
    slw_buf, olw_buf, load_sem, simg, obsg, d_ref, k_ref, x_ref,
    row_first, col_first, row_buf, col_buf, end_buf,
    send_sem, recv_sem,
):
    lines = rows_n // plane
    width, n_sim = sim_ref.shape
    n_obs = obs_ref.shape[1]
    n_i = plane * n_sim
    n_j = lines * n_obs
    r = lax.axis_index("row")
    c = lax.axis_index("col")
    z = r // plane
    q = r % plane
    group = plane * cols_n
    me = q * cols_n + c

    plane_peers = []
    for step in range(1, group):
        other = (me + step) % group
        plane_peers.append((z * plane + other // cols_n, other % cols_n))
    line_peers = []
    for step in range(1, lines):
        line_peers.append((((z + step) % lines) * plane + q, c))
    core_peers = []
    for step in range(1, plane):
        core_peers.append((z * plane + (q + step) % plane, c))

    loads = [
        pltpu.make_async_copy(sim_ref, simg.at[q, pl.ds(0, width)], load_sem.at[0]),
        pltpu.make_async_copy(obs_ref, obsg.at[z, pl.ds(0, width)], load_sem.at[1]),
        pltpu.make_async_copy(slw_ref, slw_buf, load_sem.at[2]),
        pltpu.make_async_copy(olw_ref, olw_buf, load_sem.at[3]),
    ]
    for load in loads:
        load.start()
    barrier = pltpu.get_barrier_semaphore()
    for peer in plane_peers + line_peers:
        pl.semaphore_signal(barrier, inc=1, device_id=peer, device_id_type=MESH)

    scale = LOG2E / (EPSILON * width)
    for load in loads:
        load.wait()
    x = simg[q, :width, :]
    y = obsg[z, :width, :]
    pad = simg.shape[1] - width

    def tail(values, n):
        index = lax.broadcasted_iota(jnp.int32, (pad, n), 0)
        out = jnp.zeros((pad, n), jnp.float32)
        for k, value in enumerate(values):
            if value is not None:
                out = jnp.where(index == k, jnp.broadcast_to(value, (pad, n)), out)
        return out

    one = jnp.ones((1, n_sim), jnp.float32)
    simg[q, width:, :] = tail(
        [jnp.sum(x * x, 0, keepdims=True), one, slw_buf[...]], n_sim
    )
    ones_obs = jnp.ones((1, n_obs), jnp.float32)
    obsg[z, width:, :] = tail(
        [ones_obs, jnp.sum(y * y, 0, keepdims=True), None, olw_buf[...]], n_obs
    )
    pl.semaphore_wait(barrier, len(plane_peers) + len(line_peers))

    def exchange(buf, own, peers, sem):
        for peer in peers:
            pltpu.make_async_remote_copy(
                src_ref=buf.at[own], dst_ref=buf.at[own],
                send_sem=send_sem.at[sem], recv_sem=recv_sem.at[sem],
                device_id=peer, device_id_type=MESH,
            ).start()

    def finish(buf, peers, sem):
        if peers:
            some = buf.at[pl.ds(0, len(peers))]
            pltpu.make_async_copy(some, some, recv_sem.at[sem]).wait()
            pltpu.make_async_copy(some, some, send_sem.at[sem]).wait()

    exchange(simg, q, core_peers, 1)
    exchange(obsg, z, line_peers, 0)
    finish(obsg, line_peers, 0)
    index = lax.broadcasted_iota(jnp.int32, (width + pad, n_obs), 0)
    factor = jnp.where(index < width, -2.0 * scale, scale)
    lefts = [(obsg[k] * factor).T for k in range(lines)]
    finish(simg, core_peers, 1)

    log_a = jnp.concatenate(
        [simg[k, width + 2:width + 3, :] for k in range(plane)], axis=1
    ) * LOG2E - math.log2(n_sim * rows_n)
    log_b = jnp.concatenate(
        [obsg[k, width + 3:width + 4, :] for k in range(lines)], axis=1
    ) * LOG2E - math.log2(n_obs * rows_n * cols_n)

    for k in range(lines):
        left = lefts[k]
        for m in range(plane):
            d_ref[k * n_obs:(k + 1) * n_obs, m * n_sim:(m + 1) * n_sim] = lax.dot_general(
                left, simg[m], (((1,), (0,)), ((), ())),
                precision=lax.Precision.HIGHEST, preferred_element_type=jnp.float32,
            )

    d = d_ref[...]
    low = jnp.min(d, 0, keepdims=True)
    mass = jnp.sum(jnp.exp2(low - d), 0, keepdims=True)
    row_first[me, 0:1, :] = low
    row_first[me, 1:2, :] = mass
    exchange(row_first, me, plane_peers, 2)
    finish(row_first, plane_peers, 2)

    def merge(buf, count):
        low = buf[0, 0:1, :]
        for k in range(1, count):
            low = jnp.minimum(low, buf[k, 0:1, :])
        mass = buf[0, 1:2, :] * jnp.exp2(low - buf[0, 0:1, :])
        for k in range(1, count):
            mass = mass + buf[k, 1:2, :] * jnp.exp2(low - buf[k, 0:1, :])
        return low - jnp.log2(mass)

    f = log_a + merge(row_first, group)
    scores = d_ref[...] - f
    low = jnp.min(scores, 1, keepdims=True)
    mass = jnp.sum(jnp.exp2(low - scores), 1, keepdims=True)
    col_first[z, 0:1, :] = to_row(low)
    col_first[z, 1:2, :] = to_row(mass)
    exchange(col_first, z, line_peers, 3)
    a_lifted = jnp.exp2(log_a + LIFT)
    b_lifted = jnp.exp2(log_b + LIFT)
    finish(col_first, line_peers, 3)
    g = log_b + merge(col_first, lines)

    def store_parts(ref, value, rows, parts):
        high = value.astype(jnp.bfloat16)
        ref[0, rows, :] = high
        if parts > 1:
            ref[1, rows, :] = (value - high.astype(jnp.float32)).astype(jnp.bfloat16)

    def build(f, g, last):
        parts = PARTS if last else 1
        column = to_column(g + LIFT)
        for j in range(0, n_j, 64):
            rows = pl.ds(j, 64)
            piece = column[j:j + 64]
            shift = jnp.concatenate([piece] * (n_i // 128), axis=1)
            values = jnp.exp2((f + shift) - d_ref[rows, :])
            store_parts(k_ref, values, rows, parts)
            if last:
                store_parts(x_ref, values * d_ref[rows, :], rows, 1)

    def total_of(buf, count):
        total = buf[0, 0:1, :]
        for k in range(1, count):
            total = total + buf[k, 0:1, :]
        return total

    def row_half(v_rows, parity, parts):
        buf = row_buf.at[parity]
        buf[me, 0:1, :] = matvec(v_rows, [k_ref.at[p] for p in range(parts)], 0)
        exchange(buf, me, plane_peers, 4 + parity)
        finish(buf, plane_peers, 4 + parity)
        return a_lifted / total_of(buf, group)

    def col_start(u, parity):
        buf = col_buf.at[parity]
        buf[z, 0:1, :] = matvec(split_rows(u), [k_ref.at[0]], 1)
        exchange(buf, z, line_peers, 6 + parity)

    def col_finish(parity):
        buf = col_buf.at[parity]
        finish(buf, line_peers, 6 + parity)
        return b_lifted / total_of(buf, lines)

    def block(first, f, g, v, last):
        for k in range(REBUILD):
            parity = (first + k) % 2
            u = row_half(split_rows(v), parity, 1)
            col_start(u, parity)
            if k < REBUILD - 1:
                v = col_finish(parity)
        f = f + jnp.log2(u)
        g = g + jnp.log2(v)
        build(f, g, last)
        return f, g, col_finish(parity) / v

    blocks = (ITERS - 2) // REBUILD
    assert blocks * REBUILD == ITERS - 2 and REBUILD % 2 == 0
    build(f, g, False)
    f, g, v = lax.fori_loop(
        0, blocks - 1, lambda k, carry: block(1, *carry, False),
        (f, g, jnp.ones((1, n_j), jnp.float32)),
    )
    f, g, v = block(1, f, g, v, True)

    u = row_half(split_rows(v), (ITERS - 1) % 2, PARTS)
    u_rows = split_rows(u)
    col_first[z, 0:1, :] = matvec(u_rows, [k_ref.at[p] for p in range(PARTS)], 1)
    col_first[z, 1:2, :] = matvec(u_rows, [x_ref.at[0]], 1)
    exchange(col_first, z, line_peers, 3)
    f = f + jnp.log2(u)
    f_mine = f[:, 0:n_sim]
    for k in range(1, plane):
        f_mine = jnp.where(q == k, f[:, k * n_sim:(k + 1) * n_sim], f_mine)
    out_ref[:, 0:n_sim] = f_mine * (EPSILON / LOG2E)
    finish(col_first, line_peers, 3)
    sums = col_first[0]
    for k in range(1, lines):
        sums = sums + col_first[k]
    v = b_lifted / sums[0:1]
    share = jnp.sum(v * 2.0 ** -LIFT * sums[1:2], axis=1, keepdims=True)
    end_buf[me] = jnp.broadcast_to(share * (EPSILON / LOG2E), (1, 128))
    exchange(end_buf, me, plane_peers, 8)
    g = g + jnp.log2(v)
    g_mine = g[:, 0:n_obs]
    for k in range(1, lines):
        g_mine = jnp.where(z == k, g[:, k * n_obs:(k + 1) * n_obs], g_mine)
    out_ref[:, n_sim:n_sim + n_obs] = g_mine * (EPSILON / LOG2E)
    finish(end_buf, plane_peers, 8)
    out_ref[:, n_sim + n_obs:] = total_of(end_buf, group)


def on_device(sizes, sim_points, obs_points, sim_logw, obs_logw):
    rows_n, cols_n = sizes
    plane = math.gcd(PLANE, rows_n)
    lines = rows_n // plane
    group = plane * cols_n
    width, n_sim = sim_points.shape
    n_obs = obs_points.shape[1]
    n_i, n_j = plane * n_sim, lines * n_obs
    f32, bf16 = jnp.float32, jnp.bfloat16
    depth = -(-width // 8) * 8 + 8
    assert width % 8 == 0
    vmem = pl.BlockSpec(memory_space=pltpu.VMEM)
    out = pl.pallas_call(
        functools.partial(body, rows_n, cols_n, plane),
        out_shape=jax.ShapeDtypeStruct((1, n_sim + n_obs + 128), f32),
        in_specs=[pl.BlockSpec(memory_space=pltpu.HBM)] * 4,
        out_specs=vmem,
        scratch_shapes=[
            pltpu.VMEM((1, n_sim), f32),
            pltpu.VMEM((1, n_obs), f32),
            pltpu.SemaphoreType.DMA((4,)),
            pltpu.VMEM((plane, depth, n_sim), f32),
            pltpu.VMEM((lines, depth, n_obs), f32),
            pltpu.VMEM((n_j, n_i), f32),
            pltpu.VMEM((PARTS, n_j, n_i), bf16),
            pltpu.VMEM((1, n_j, n_i), bf16),
            pltpu.VMEM((group, 2, n_i), f32),
            pltpu.VMEM((lines, 2, n_j), f32),
            pltpu.VMEM((2, group, 1, n_i), f32),
            pltpu.VMEM((2, lines, 1, n_j), f32),
            pltpu.VMEM((group, 1, 128), f32),
            pltpu.SemaphoreType.DMA((9,)),
            pltpu.SemaphoreType.DMA((9,)),
        ],
        compiler_params=pltpu.CompilerParams(
            collective_id=0, has_side_effects=True, vmem_limit_bytes=57 * 2**20
        ),
        name="sinkhorn",
    )(sim_points, obs_points, sim_logw[None, :], obs_logw[None, :])
    out = out[0]
    return out[:n_sim], out[n_sim:n_sim + n_obs], out[n_sim + n_obs:n_sim + n_obs + 1]


def solution(mesh):
    P = jax.sharding.PartitionSpec
    in_specs = (P(None, "row"), P(None, ("row", "col")), P("row"), P(("row", "col")))
    out_specs = (P("row"), P(("row", "col")), P())
    sizes = (mesh.shape["row"], mesh.shape["col"])
    return jax.shard_map(
        functools.partial(on_device, sizes),
        mesh=mesh, in_specs=in_specs, out_specs=out_specs, check_vma=False,
    )
```
